256 devices in a mesh: dp: 4 (over y), expert: 64 (over z, x, core).
Axes of the slice: x: 4, y: 4, z: 8, core: 2. Of those that a mesh axis runs over, the one named last changes fastest.
Arguments:
- tokens: bfloat16 [32768, 2048], P(('dp', 'expert')), may hold values from -6 to 6
- cotangent: bfloat16 [32768, 2048], P(('dp', 'expert')), may hold values from -3 to 3
- routes: int32 [32768, 1], P(('dp', 'expert')), may hold values from 0 to 63, as said below
- gate_fixed: int32 [32768, 1], P(('dp', 'expert')), may hold values from 8192 to 65535
- w_gate: bfloat16 [64, 2048, 768], P('expert', 'dp'), may hold values from -0.125 to 0.125
- w_up: bfloat16 [64, 2048, 768], P('expert', 'dp'), may hold values from -0.125 to 0.125
- w_down: bfloat16 [64, 768, 2048], P('expert', None, 'dp'), may hold values from -0.21875 to 0.21875
Outputs:
- mixed: bfloat16 [32768, 2048], P(('dp', 'expert'))
- grad_tokens: bfloat16 [32768, 2048], P(('dp', 'expert'))
- grad_w_gate: bfloat16 [64, 2048, 768], P('expert', 'dp')
- grad_w_up: bfloat16 [64, 2048, 768], P('expert', 'dp')
- grad_w_down: bfloat16 [64, 768, 2048], P('expert', None, 'dp')
The draws below stay inside these ranges and needn't reach their ends.
Inputs may be any that keep to these rules, and one draw needn't show every extreme that they name: `routes`: each token names one expert. Among the tokens of one device no expert is named more than 3 times, and some experts are named exactly 3 times by the tokens of every device.
All inputs are finite; a program needn't handle non-finite values.
Results may differ from the reference program's by a relative error of at most 0.0058.
Values may be sent and summed in bfloat16 or wider, within the bound.
A program may use at most 64 MiB of HBM per device.

```python
import jax
import jax.numpy as jnp
from jax import lax

D = 2048
FF = 768
TOP = 1
TOK_DEV = 128
EXPERTS = 64
CAP = 3
TOKENS = 32768


def draw_routes(key, part):
    blocks = TOKENS // TOK_DEV
    slot_total = TOK_DEV * TOP
    half_load = slot_total // (2 * EXPERTS)
    groups = EXPERTS // 4
    key_order, key_share, key_place = jax.random.split(jax.random.fold_in(key, 7), 3)
    ranked = jax.random.permutation(key_order, EXPERTS).astype(jnp.int32)
    scores = jax.random.randint(key_share, (blocks, groups, 3), 0, 1 << 16) * 4 + jnp.arange(3, dtype=jnp.int32)
    picks = jnp.argsort(scores, axis=2)
    others = jnp.array([2, 2, 1], jnp.int32)[picks]
    leaders = jnp.full((blocks, groups, 1), 3, jnp.int32)
    quota = jnp.concatenate([leaders, others], axis=2).reshape(blocks, EXPERTS) * half_load
    bounds = jnp.cumsum(quota, axis=1)
    position = jnp.arange(slot_total, dtype=jnp.int32)
    rank_of = jnp.sum((bounds[:, None, :] <= position[None, :, None]).astype(jnp.int32), axis=2)
    chosen = ranked[rank_of]
    chosen = jnp.transpose(chosen.reshape(blocks, TOP, TOK_DEV), (0, 2, 1))
    place_scores = jax.random.randint(key_place, (blocks, TOK_DEV), 0, 1 << 16) * TOK_DEV + jnp.arange(TOK_DEV, dtype=jnp.int32)
    shuffle = jnp.argsort(place_scores, axis=1)
    chosen = jnp.take_along_axis(chosen, shuffle[:, :, None], axis=1)
    return chosen.reshape(TOKENS, TOP).astype(jnp.int32)


def with_ends(values, own_key, least, top_value):
    longest = values.shape.index(max(values.shape))
    spots = []
    for shift in (0, 1):
        where = [jax.random.randint(jax.random.fold_in(own_key, axis), (), 0, length) for axis, length in enumerate(values.shape)]
        where[longest] = (where[longest] + shift) % values.shape[longest]
        spots.append(tuple(where))
    return values.at[spots[0]].set(least).at[spots[1]].set(top_value)


def levels(own_key, shape, shards, smallest, largest):
    def one(dim, parts):
        steps = jax.random.uniform(jax.random.fold_in(jax.random.fold_in(own_key, 6), dim), (parts,), jnp.float32, smallest / len(shards), largest / len(shards))
        return jnp.repeat(jnp.exp(steps), shape[dim] // parts).reshape((-1,) + (1,) * (len(shape) - dim - 1))

    level = one(*shards[0])
    for cut in shards[1:]:
        level = level * one(*cut)
    return level


def normal_values(rng, extent, scale, most, cuts=(), kind=jnp.bfloat16):
    values = jax.random.normal(rng, extent, jnp.float32) * scale
    if len(cuts) > 0:
        values = levels(rng, extent, cuts, -0.22, 0.18) * values
    return jnp.clip(values, min=-most, max=most).astype(kind)


def setup_inputs(seed: int = 0) -> dict:
    streams_of = jax.random.split(jax.random.key(seed), 8)
    return {
        "tokens": normal_values(streams_of[0], (TOKENS, D), 1.0, 6.0, ((0, 256),)),
        "cotangent": normal_values(streams_of[1], (TOKENS, D), 0.5, 3.0, ((0, 256),)),
        "routes": draw_routes(jax.random.fold_in(streams_of[7], 71), 0),
        "gate_fixed": with_ends(jax.random.randint(streams_of[3], (TOKENS, TOP), 8192, 65536), jax.random.fold_in(streams_of[3], 1), 8192, 65535).astype(jnp.int32),
        "w_gate": normal_values(streams_of[4], (EXPERTS, D, FF), D ** -0.5, 0.125, ((0, 64), (1, 4))),
        "w_up": normal_values(streams_of[5], (EXPERTS, D, FF), D ** -0.5, 0.125, ((0, 64), (1, 4))),
        "w_down": normal_values(streams_of[6], (EXPERTS, FF, D), FF ** -0.5, 0.21875, ((0, 64), (2, 4))),
    }


def slot_index(routes):
    blocks = TOKENS // TOK_DEV
    per_block = routes.reshape(blocks, TOK_DEV * TOP)
    one_hot = (per_block[:, :, None] == jnp.arange(EXPERTS, dtype=jnp.int32)[None, None, :]).astype(jnp.int32)
    earlier = jnp.cumsum(one_hot, axis=1) - one_hot
    position = jnp.sum(earlier * one_hot, axis=2)
    block_id = jnp.arange(blocks, dtype=jnp.int32)[:, None]
    return ((per_block * blocks + block_id) * CAP + position).reshape(TOKENS * TOP).astype(jnp.int32)


def reference(tokens, cotangent, routes, gate_fixed, w_gate, w_up, w_down):
    blocks = TOKENS // TOK_DEV
    all_slots = EXPERTS * blocks * CAP
    route_weight = gate_fixed.astype(jnp.float32) / 65536.0
    index = slot_index(routes)
    route_rows = (jnp.arange(TOKENS * TOP, dtype=jnp.int32) // TOP).astype(jnp.int32)
    source_row = jnp.zeros((all_slots,), jnp.int32).at[index].set(route_rows)
    occupied = jnp.zeros((all_slots,), jnp.int32).at[index].set(1)
    slot_weight = jnp.zeros((all_slots,), jnp.float32).at[index].set(route_weight.reshape(TOKENS * TOP))
    source_row = source_row.reshape(EXPERTS, blocks * CAP)
    occupied = occupied.reshape(EXPERTS, blocks * CAP)
    slot_weight = slot_weight.reshape(EXPERTS, blocks * CAP)

    def expert_pass(inputs):
        gate_w, up_w, down_w, rows_here, filled, scale_here = inputs
        keep = filled[:, None] > 0
        inputs_here = jnp.where(keep, tokens[rows_here], jnp.zeros((), tokens.dtype))
        scaled = (scale_here[:, None] * cotangent[rows_here].astype(jnp.float32)).astype(jnp.bfloat16)
        grads_here = jnp.where(keep, scaled, jnp.zeros((), scaled.dtype))
        gate_pre = jnp.dot(inputs_here, gate_w, preferred_element_type=jnp.float32)
        up_pre = jnp.dot(inputs_here, up_w, preferred_element_type=jnp.float32)
        sigmoid_gate = jax.nn.sigmoid(gate_pre)
        hidden = (gate_pre * sigmoid_gate * up_pre).astype(jnp.bfloat16)
        outputs_here = jnp.dot(hidden, down_w, preferred_element_type=jnp.float32).astype(jnp.bfloat16)
        grad_hidden = lax.dot_general(grads_here, down_w, (((1,), (1,)), ((), ())), preferred_element_type=jnp.float32)
        grad_gate = (grad_hidden * up_pre * sigmoid_gate * (1.0 + gate_pre * (1.0 - sigmoid_gate))).astype(jnp.bfloat16)
        grad_up = (grad_hidden * gate_pre * sigmoid_gate).astype(jnp.bfloat16)
        grad_inputs = (lax.dot_general(grad_gate, gate_w, (((1,), (1,)), ((), ())), preferred_element_type=jnp.float32)
                       + lax.dot_general(grad_up, up_w, (((1,), (1,)), ((), ())), preferred_element_type=jnp.float32)).astype(jnp.bfloat16)
        grad_gate_w = lax.dot_general(inputs_here, grad_gate, (((0,), (0,)), ((), ())), preferred_element_type=jnp.float32).astype(jnp.bfloat16)
        grad_up_w = lax.dot_general(inputs_here, grad_up, (((0,), (0,)), ((), ())), preferred_element_type=jnp.float32).astype(jnp.bfloat16)
        grad_down_w = lax.dot_general(hidden, grads_here, (((0,), (0,)), ((), ())), preferred_element_type=jnp.float32).astype(jnp.bfloat16)
        return outputs_here, grad_inputs, grad_gate_w, grad_up_w, grad_down_w

    slot_out, slot_grad_in, grad_w_gate, grad_w_up, grad_w_down = lax.map(
        expert_pass, (w_gate, w_up, w_down, source_row, occupied, slot_weight))
    slot_out = slot_out.reshape(all_slots, D)
    slot_grad_in = slot_grad_in.reshape(all_slots, D)
    picked = slot_out[index].reshape(TOKENS, TOP, D).astype(jnp.float32)
    mixed = jnp.sum(route_weight[:, :, None] * picked, axis=1).astype(jnp.bfloat16)
    grad_tokens = jnp.sum(slot_grad_in[index].reshape(TOKENS, TOP, D).astype(jnp.float32), axis=1).astype(jnp.bfloat16)
    return mixed, grad_tokens, grad_w_gate, grad_w_up, grad_w_down
```

```python
import functools

import jax
import jax.numpy as jnp
from jax import lax
from jax.experimental import pallas as pl
from jax.experimental.pallas import tpu as pltpu
from jax.sharding import Mesh
from jax.sharding import PartitionSpec as P

AXES = ("dp", "e_z", "e_x", "e_c")
EXPERT = ("e_z", "e_x", "e_c")
SLOTS = 3
MESH_ID = pl.DeviceIdType.MESH
BF16 = jnp.bfloat16
F32 = jnp.float32


def dot(a, b, dims=((1,), (0,))):
    return lax.dot_general(a, b, (dims, ((), ())), preferred_element_type=F32)


def layer_kernel(
    sizes,
    routes_ref, gate_ref, tok_ref, cot_ref, wg_ref, wu_ref, wd_ref,
    mixed_ref, gtok_ref, gwg_ref, gwu_ref, gwd_ref,
    xs, xb, xa, xc, gs, gb, ga, gc, ys, ya, yb, yc, ds, da, db, dc,
    perm, wgt, wut, wdt,
    gu_send, gu_recv, gu, gh_send, gh_recv, gh, hid, ggu,
    send_sem, recv_sem, dp_send, dp_recv,
):
    ny, nz, nx, nc = sizes
    na, nb = nz * nc, ny * nx
    tok_count, width = tok_ref.shape
    part = width // ny
    ff = wg_ref.shape[1]
    rows = na * nb * SLOTS
    own = rows // ny
    per = na // ny
    y, z, x, c = (lax.axis_index(a) for a in AXES)
    my_a = z * nc + c
    my_b = y * nx + x

    def dev_a(i):
        return (y, i // nc, x, lax.rem(i, nc))

    def dev_b(i):
        return (i // nx, z, lax.rem(i, nx), c)

    def dev_y(i):
        return (i, z, x, c)

    barrier = pltpu.get_barrier_semaphore()

    @pl.loop(1, na)
    def _(o):
        pl.semaphore_signal(barrier, inc=1, device_id=dev_a(lax.rem(my_a + o, na)), device_id_type=MESH_ID)

    @pl.loop(1, nb)
    def _(o):
        pl.semaphore_signal(barrier, inc=1, device_id=dev_b(lax.rem(my_b + o, nb)), device_id_type=MESH_ID)

    def copy_of(phase, src, dst, me, peer, o, dev):
        return pltpu.make_async_remote_copy(
            src_ref=src.at[peer], dst_ref=dst.at[me],
            send_sem=send_sem.at[phase, o], recv_sem=recv_sem.at[phase, me],
            device_id=dev(peer), device_id_type=MESH_ID,
        )

    def start_all(phase, src, dst, me, count, dev):
        @pl.loop(1, count)
        def _(o):
            copy_of(phase, src, dst, me, lax.rem(me + o, count), o, dev).start()
        dst[me] = src[me]

    def wait_recv(phase, src, dst, me, count, dev):
        @pl.loop(1, count)
        def _(o):
            s = lax.rem(me + o, count)
            pltpu.make_async_remote_copy(
                src_ref=src.at[s], dst_ref=dst.at[s],
                send_sem=send_sem.at[phase, o], recv_sem=recv_sem.at[phase, s],
                device_id=dev(s), device_id_type=MESH_ID,
            ).wait_recv()

    def wait_send(phase, src, dst, me, count, dev):
        @pl.loop(1, count)
        def _(o):
            copy_of(phase, src, dst, me, lax.rem(me + o, count), o, dev).wait_send()

    def dp_copy(kind, src, dst, o):
        return pltpu.make_async_remote_copy(
            src_ref=src, dst_ref=dst, send_sem=dp_send.at[kind, o], recv_sem=dp_recv.at[kind, o],
            device_id=dev_y(lax.rem(y + o, ny)), device_id_type=MESH_ID,
        )

    lane = lax.broadcasted_iota(jnp.int32, (tok_count, tok_count), 1)
    sub = lax.broadcasted_iota(jnp.int32, (tok_count, tok_count), 0)
    diag = lane == sub
    r_row = jnp.broadcast_to(routes_ref[...], (tok_count, tok_count))
    r_col = jnp.sum(jnp.where(diag, r_row, 0), axis=1, keepdims=True)
    same = r_row == r_col
    k_row = jnp.sum(jnp.where(same & (sub < lane), 1, 0), axis=0, keepdims=True)
    k_col = jnp.sum(jnp.where(same & (lane < sub), 1, 0), axis=1, keepdims=True)

    def place(r, k):
        rz, rx, rc = r // (nx * nc), lax.rem(r // nc, nx), lax.rem(r, nc)
        return rx * (na * SLOTS) + (rz * nc + rc) * SLOTS + k

    own_slots = nx * na * SLOTS
    base_row = place(routes_ref[...], k_row)
    base_col = place(r_col, k_col)
    pick_in = (lax.broadcasted_iota(jnp.int32, (own_slots, tok_count), 0) == base_row).astype(F32).astype(BF16)
    pick_out = (lax.broadcasted_iota(jnp.int32, (tok_count, own_slots), 1) == base_col).astype(F32).astype(BF16)
    weight = gate_ref[...].astype(F32) / 65536.0
    w_col = jnp.sum(jnp.where(diag, jnp.broadcast_to(weight, (tok_count, tok_count)), 0.0), axis=1, keepdims=True)

    for j in range(ny):
        cols = tok_ref[:, j * part:(j + 1) * part]
        xs[j * nx:(j + 1) * nx] = dot(pick_in, cols).astype(BF16).reshape(nx, na * SLOTS, part)

    pl.semaphore_wait(barrier, na + nb - 2)
    start_all(0, xs, xb, my_b, nb, dev_b)

    for j in range(ny):
        cols = (w_col * cot_ref[:, j * part:(j + 1) * part].astype(F32)).astype(BF16)
        gs[j * nx:(j + 1) * nx] = dot(pick_in, cols).astype(BF16).reshape(nx, na * SLOTS, part)

    start_all(1, gs, gb, my_b, nb, dev_b)

    n = lax.broadcasted_iota(jnp.int32, (rows, 128), 0)
    inner = lax.rem(n, na * SLOTS)
    source = (inner // SLOTS) * (nb * SLOTS) + (n // (na * SLOTS)) * SLOTS + lax.rem(inner, SLOTS)
    step = min(128, rows)
    for q in range(rows // step):
        at = lax.broadcasted_iota(jnp.int32, (rows, step), 1) + q * step
        perm[:, q * step:(q + 1) * step] = (at == source[:, :step]).astype(F32).astype(BF16)

    def turned(src, dst):
        @pl.loop(0, ny)
        def _(q):
            lines = perm[pl.ds(pl.multiple_of(q * own, own), own), :]
            dst[pl.ds(q * per, per)] = dot(lines, src[...].reshape(rows, part)).astype(BF16).reshape(per, nb * SLOTS, part)

    wgt[...] = wg_ref[...].T
    wut[...] = wu_ref[...].T
    wdt[...] = wd_ref[...].T

    wait_recv(0, xs, xb, my_b, nb, dev_b)
    turned(xb, xa)
    start_all(2, xa, xc, my_a, na, dev_a)

    wait_recv(1, gs, gb, my_b, nb, dev_b)
    turned(gb, ga)
    start_all(3, ga, gc, my_a, na, dev_a)

    def block(ref, q):
        return ref[pl.ds(q * per, per)].reshape(own, part)

    wait_recv(2, xa, xc, my_a, na, dev_a)

    @pl.loop(1, ny)
    def _(o):
        lines = block(xc, lax.rem(y + o, ny))
        gu_send[o - 1, :, :ff] = dot(lines, wg_ref[...]).astype(BF16)
        gu_send[o - 1, :, ff:] = dot(lines, wu_ref[...]).astype(BF16)
        dp_copy(0, gu_send.at[o - 1], gu_recv.at[o - 1], o).start()

    lines = block(xc, y)
    gu[:, :ff] = dot(lines, wg_ref[...])
    gu[:, ff:] = dot(lines, wu_ref[...])

    wait_recv(3, ga, gc, my_a, na, dev_a)

    @pl.loop(1, ny)
    def _(o):
        gh_send[o - 1] = dot(block(gc, lax.rem(y + o, ny)), wdt[...]).astype(BF16)
        dp_copy(1, gh_send.at[o - 1], gh_recv.at[o - 1], o).start()

    gh[...] = dot(block(gc, y), wdt[...])

    @pl.loop(1, ny)
    def _(o):
        dp_copy(0, gu_send.at[o - 1], gu_recv.at[o - 1], o).wait_recv()

    chunk = min(16, own)

    @pl.loop(0, own // chunk)
    def _(i):
        at = pl.ds(pl.multiple_of(i * chunk, chunk), chunk)
        total = gu[at, :]
        for o in range(ny - 1):
            total += gu_recv[o, at, :].astype(F32)
        gu[at, :] = total
        gate, up = total[:, :ff], total[:, ff:]
        hid[y, at, :] = (gate * jax.nn.sigmoid(gate) * up).astype(BF16)

    @pl.loop(1, ny)
    def _(o):
        dp_copy(2, hid.at[y], hid.at[y], o).start()

    @pl.loop(1, ny)
    def _(o):
        dp_copy(1, gh_send.at[o - 1], gh_recv.at[o - 1], o).wait_recv()

    @pl.loop(0, own // chunk)
    def _(i):
        at = pl.ds(pl.multiple_of(i * chunk, chunk), chunk)
        grad = gh[at, :]
        for o in range(ny - 1):
            grad += gh_recv[o, at, :].astype(F32)
        gate, up = gu[at, :ff], gu[at, ff:]
        s = jax.nn.sigmoid(gate)
        ggu[y, at, :ff] = (grad * up * s * (1.0 + gate * (1.0 - s))).astype(BF16)
        ggu[y, at, ff:] = (grad * gate * s).astype(BF16)

    @pl.loop(1, ny)
    def _(o):
        dp_copy(3, ggu.at[y], ggu.at[y], o).start()

    def down(q):
        ys[pl.ds(q * per, per)] = dot(hid[q], wd_ref[...]).astype(BF16).reshape(per, nb * SLOTS, part)

    def back(q):
        total = dot(ggu[q, :, :ff], wgt[...]) + dot(ggu[q, :, ff:], wut[...])
        ds[pl.ds(q * per, per)] = total.astype(BF16).reshape(per, nb * SLOTS, part)

    def from_dp(kind, buf, work):
        @pl.loop(0, ny)
        def _(o):
            q = lax.rem(y + ny - o, ny)

            @pl.when(o > 0)
            def _():
                dp_copy(kind, buf.at[q], buf.at[q], o).wait_recv()
            work(q)

    from_dp(2, hid, down)
    start_all(4, ys, ya, my_a, na, dev_a)
    from_dp(3, ggu, back)
    start_all(5, ds, da, my_a, na, dev_a)

    wait_recv(4, ys, ya, my_a, na, dev_a)
    turned(ya, yb)
    start_all(6, yb, yc, my_b, nb, dev_b)

    tn = ((0,), (0,))
    step = min(256, ff)
    for f in range(ff // step):
        cut = slice(f * step, (f + 1) * step)
        gwg_ref[:, cut] = dot(xc[...].reshape(rows, part), ggu[:, :, cut].reshape(rows, step), tn).astype(BF16)

    wait_recv(5, ds, da, my_a, na, dev_a)
    turned(da, db)
    start_all(7, db, dc, my_b, nb, dev_b)

    for f in range(ff // step):
        cut = slice(f * step, (f + 1) * step)
        high = slice(ff + f * step, ff + (f + 1) * step)
        gwu_ref[:, cut] = dot(xc[...].reshape(rows, part), ggu[:, :, high].reshape(rows, step), tn).astype(BF16)
        gwd_ref[cut, :] = dot(hid[:, :, cut].reshape(rows, step), gc[...].reshape(rows, part), tn).astype(BF16)

    wait_recv(6, yb, yc, my_b, nb, dev_b)
    for j in range(ny):
        picked = dot(pick_out, yc[j * nx:(j + 1) * nx].reshape(own_slots, part))
        mixed_ref[:, j * part:(j + 1) * part] = (w_col * picked).astype(BF16)

    wait_recv(7, db, dc, my_b, nb, dev_b)
    for j in range(ny):
        picked = dot(pick_out, dc[j * nx:(j + 1) * nx].reshape(own_slots, part))
        gtok_ref[:, j * part:(j + 1) * part] = picked.astype(BF16)

    wait_send(0, xs, xb, my_b, nb, dev_b)
    wait_send(1, gs, gb, my_b, nb, dev_b)
    wait_send(2, xa, xc, my_a, na, dev_a)
    wait_send(3, ga, gc, my_a, na, dev_a)
    wait_send(4, ys, ya, my_a, na, dev_a)
    wait_send(5, ds, da, my_a, na, dev_a)
    wait_send(6, yb, yc, my_b, nb, dev_b)
    wait_send(7, db, dc, my_b, nb, dev_b)

    @pl.loop(1, ny)
    def _(o):
        dp_copy(0, gu_send.at[o - 1], gu_recv.at[o - 1], o).wait_send()
        dp_copy(1, gh_send.at[o - 1], gh_recv.at[o - 1], o).wait_send()
        dp_copy(2, hid.at[y], hid.at[y], o).wait_send()
        dp_copy(3, ggu.at[y], ggu.at[y], o).wait_send()


def body(sizes, tokens, cotangent, routes, gate_fixed, w_gate, w_up, w_down):
    ny, nz, nx, nc = sizes
    na, nb = nz * nc, ny * nx
    tok_count, width = tokens.shape
    ff = w_gate.shape[2]
    part = width // ny
    rows = na * nb * SLOTS
    own = rows // ny
    by_b = pltpu.VMEM((nb, na * SLOTS, part), BF16)
    by_a = pltpu.VMEM((na, nb * SLOTS, part), BF16)
    vmem = pl.BlockSpec(memory_space=pltpu.VMEM)
    outs = pl.pallas_call(
        functools.partial(layer_kernel, sizes),
        out_shape=(
            jax.ShapeDtypeStruct((tok_count, width), BF16),
            jax.ShapeDtypeStruct((tok_count, width), BF16),
            jax.ShapeDtypeStruct((part, ff), BF16),
            jax.ShapeDtypeStruct((part, ff), BF16),
            jax.ShapeDtypeStruct((ff, part), BF16),
        ),
        in_specs=[vmem] * 7,
        out_specs=(vmem,) * 5,
        scratch_shapes=[
            by_b, by_b, by_a, by_a, by_b, by_b, by_a, by_a,
            by_a, by_a, by_b, by_b, by_a, by_a, by_b, by_b,
            pltpu.VMEM((rows, rows), BF16),
            pltpu.VMEM((ff, part), BF16),
            pltpu.VMEM((ff, part), BF16),
            pltpu.VMEM((part, ff), BF16),
            pltpu.VMEM((ny - 1, own, 2 * ff), BF16),
            pltpu.VMEM((ny - 1, own, 2 * ff), BF16),
            pltpu.VMEM((own, 2 * ff), F32),
            pltpu.VMEM((ny - 1, own, ff), BF16),
            pltpu.VMEM((ny - 1, own, ff), BF16),
            pltpu.VMEM((own, ff), F32),
            pltpu.VMEM((ny, own, ff), BF16),
            pltpu.VMEM((ny, own, 2 * ff), BF16),
            pltpu.SemaphoreType.DMA((8, max(na, nb))),
            pltpu.SemaphoreType.DMA((8, max(na, nb))),
            pltpu.SemaphoreType.DMA((4, ny)),
            pltpu.SemaphoreType.DMA((4, ny)),
        ],
        compiler_params=pltpu.CompilerParams(
            collective_id=0, has_side_effects=True, vmem_limit_bytes=60 * 2**20
        ),
    )(
        routes.reshape(1, tok_count), gate_fixed.reshape(1, tok_count), tokens, cotangent,
        w_gate[0], w_up[0], w_down[0],
    )
    mixed, grad_tokens, grad_w_gate, grad_w_up, grad_w_down = outs
    return mixed, grad_tokens, grad_w_gate[None], grad_w_up[None], grad_w_down[None]


def solution(mesh, split=(8, 4, 2)):
    sizes = (mesh.shape["dp"],) + split
    finer = Mesh(mesh.devices.reshape(sizes), AXES)
    tok = P(AXES, None)
    return jax.shard_map(
        functools.partial(body, sizes),
        mesh=finer,
        in_specs=(tok, tok, tok, tok, P(EXPERT, "dp", None), P(EXPERT, "dp", None), P(EXPERT, None, "dp")),
        out_specs=(tok, tok, P(EXPERT, "dp", None), P(EXPERT, "dp", None), P(EXPERT, None, "dp")),
        check_vma=False,
    )
```
